32 devices in a mesh: groups: 2 (over y), row: 4 (over z), col: 2 (over x), mode: 2 (over core).
Axes of the slice: x: 2, y: 2, z: 4, core: 2. Of those that a mesh axis runs over, the one named last changes fastest.
Arguments:
- object_field: float32 [2048, 2, 1024], P(('groups', 'row'), None, 'col'), parts along dimension 0, may hold values from -12 to 12
- probe_field: float32 [512, 2, 256], P('groups'), parts along dimension 0, may hold values from -5 to 5
- amplitudes: bfloat16 [128, 256, 256], P(('groups', 'row', 'col', 'mode')), parts along dimension 0
- row_offset: int32 [128], P(('groups', 'row', 'col', 'mode')), parts along dimension 0, may hold values from 0 to 768, as said below
- col_offset: int32 [128], P(('groups', 'row', 'col', 'mode')), parts along dimension 0, may hold values from 0 to 768, as said below
- counts: int32 [32], P(('groups', 'row', 'col', 'mode')), parts along dimension 0, may hold values from 1 to 4
Outputs:
- object_new: float32 [2048, 2, 1024], P(('groups', 'row', 'mode'), None, 'col'), parts along dimension 0
- probe_new: float32 [512, 2, 256], P('groups'), parts along dimension 0
The draws below stay inside these ranges and needn't reach their ends.
There are 2 independent parts, one for each index of `groups`. The reference program is written for one: setup_inputs(seed, part) draws one part's arguments, and reference() takes and returns one part's arrays. A program takes and returns all parts, laid end to end along the dimension named above; each array names one. Nothing has to cross between parts.
Inputs may be any that keep to these rules, and one draw needn't show every extreme that they name: `row_offset`: slot j lies on device j div 4 of row+col+mode; its patch starts inside that device's object tile of 256 rows, on a multiple of 64, and stays inside the object. `col_offset`: its patch starts inside the device's tile of 512 columns, on a multiple of 64, and stays inside the object.
All inputs are finite; a program needn't handle non-finite values.
Results may differ from the reference program's by a relative error of at most 0.0007.
The reference program's roundings to bfloat16 on the way count: a program that leaves them out, or rounds other values in their place, can miss the bound.
Values may be sent and summed in bfloat16 or wider, within the bound.
A program may use at most 64 MiB of HBM per device.

```python
import math
import jax
import jax.numpy as jnp
from jax import lax

FRAME = 256
TILE_R = 256
TILE_C = 512
POS_DEV = 4
OBJ_R = 1024
OBJ_C = 1024
DEV_PART = 16
POSITIONS = 64


def offsets_within(key, device_ids, slot_within, tile_ids, tiles_count, extent):
    raster_step = FRAME // 4
    limit = jnp.where(tile_ids == tiles_count - 1, extent - FRAME + 1, extent).astype(jnp.int32)
    points = ((limit - 1) // raster_step + 1).astype(jnp.int32)
    raw_index = jax.random.randint(jax.random.fold_in(key, 1), device_ids.shape, 0, points).astype(jnp.int32)
    favored = jax.random.randint(jax.random.fold_in(key, 3), (), 0, 4).astype(jnp.int32)
    take_favored = jax.random.randint(jax.random.fold_in(key, 4), device_ids.shape, 0, 2) == 1
    aligned = favored + 4 * (raw_index // 4)
    index = jnp.where(take_favored & (aligned < points), aligned, raw_index)
    picks = jax.random.randint(jax.random.fold_in(key, 2), (DEV_PART,), 0, POS_DEV).astype(jnp.int32)
    chosen = picks[device_ids]
    index = jnp.where(slot_within == chosen, points - 1, index)
    index = jnp.where(slot_within == (chosen + 1) % POS_DEV, 0, index)
    return (tile_ids * extent + index * raster_step).astype(jnp.int32)


def draw_row_offset(key, part):
    slot_ids = jnp.arange(POSITIONS, dtype=jnp.int32)
    device_ids = slot_ids // POS_DEV
    rows_count = OBJ_R // TILE_R
    per_row = DEV_PART // rows_count
    tile_ids = device_ids // per_row
    return offsets_within(jax.random.fold_in(key, 11), device_ids, slot_ids % POS_DEV, tile_ids, rows_count, TILE_R)


def draw_col_offset(key, part):
    slot_ids = jnp.arange(POSITIONS, dtype=jnp.int32)
    device_ids = slot_ids // POS_DEV
    rows_count = OBJ_R // TILE_R
    cols_count = OBJ_C // TILE_C
    modes_count = DEV_PART // (rows_count * cols_count)
    tile_ids = device_ids // modes_count % cols_count
    return offsets_within(jax.random.fold_in(key, 12), device_ids, slot_ids % POS_DEV, tile_ids, cols_count, TILE_C)


def draw_counts(key, part):
    first_draw = jax.random.randint(jax.random.fold_in(key, 21), (DEV_PART,), 0, POS_DEV)
    second_draw = jax.random.randint(jax.random.fold_in(key, 22), (DEV_PART,), 0, POS_DEV)
    base_count = 1 + jnp.minimum(first_draw, second_draw)
    phase_pick = jax.random.randint(jax.random.fold_in(key, 23), (), 0, 8)
    device_ids = jnp.arange(DEV_PART, dtype=jnp.int32)
    return jnp.where(device_ids % 8 == phase_pick, POS_DEV, base_count).astype(jnp.int32)


def draw_amplitudes(key, part):
    position_frac = jnp.arange(POSITIONS, dtype=jnp.float32) / max(POSITIONS - 1, 1)
    frame_gain = jax.random.uniform(jax.random.fold_in(key, 31), (POSITIONS, 1, 1), minval=0.7, maxval=1.4)
    ramp_values = 1.0 + 2.0 * position_frac
    normal_values = jnp.clip(jax.random.normal(jax.random.fold_in(key, 33), (POSITIONS, FRAME, FRAME)), -5.0, 5.0)
    values = jnp.abs(normal_values) * 1.25
    return (values * frame_gain * ramp_values[:, None, None]).astype(jnp.bfloat16)


def draw_object_field(key, part):
    normal_values = jnp.clip(jax.random.normal(jax.random.fold_in(key, 41), (OBJ_R, 2, OBJ_C)), -5.0, 5.0) * 0.7
    return normal_values.astype(jnp.float32)


def noise(own_key, shape, deviation, bound, kind=jnp.bfloat16):
    entries = jax.random.normal(own_key, shape, jnp.float32) * deviation
    return jnp.minimum(jnp.maximum(entries, -bound), bound).astype(kind)


def setup_inputs(seed: int = 0, part: int = 0) -> dict:
    arg_keys = jax.random.split(jax.random.key(seed), 7)
    part_keys = jax.random.split(jax.random.fold_in(arg_keys[6], part), 7)
    return {
        "object_field": draw_object_field(jax.random.fold_in(jax.random.fold_in(arg_keys[6], part), 71), part),
        "probe_field": noise(part_keys[1], (FRAME, 2, FRAME), 0.7, 5.0, jnp.float32),
        "amplitudes": draw_amplitudes(jax.random.fold_in(jax.random.fold_in(arg_keys[6], part), 71), part),
        "row_offset": draw_row_offset(jax.random.fold_in(jax.random.fold_in(arg_keys[6], part), 71), part),
        "col_offset": draw_col_offset(jax.random.fold_in(jax.random.fold_in(arg_keys[6], part), 71), part),
        "counts": draw_counts(jax.random.fold_in(jax.random.fold_in(arg_keys[6], part), 71), part),
    }


MODULUS_FLOOR = 0.5
EPSILON = 1e-05
REGULARIZER = 1.0

def dft_table(points, sign):
    freq_index = jnp.arange(points, dtype=jnp.int32)
    product = freq_index[:, None] * freq_index[None, :] % points
    angle_grid = 2.0 * math.pi / points * product.astype(jnp.float32)
    norm_factor = 1.0 / math.sqrt(points)
    cosine = jnp.cos(angle_grid) * norm_factor
    sine_part = jnp.sin(angle_grid) * (sign * norm_factor)
    upper_rows = jnp.stack([cosine, sine_part], axis=-1)
    lower_rows = jnp.stack([-sine_part, cosine], axis=-1)
    return jnp.stack([upper_rows, lower_rows], axis=1).astype(jnp.bfloat16)

def transform(frames, dft_matrix):
    wide_table = dft_matrix.astype(jnp.float32)
    frames = lax.optimization_barrier(frames)
    first_pass = jnp.einsum('kanb,nbm->kam', wide_table, frames.astype(jnp.float32), precision=lax.Precision.HIGHEST)
    first_pass = lax.optimization_barrier(first_pass.astype(jnp.bfloat16)).astype(jnp.float32)
    return jnp.einsum('kbm,lamb->kal', first_pass, wide_table, precision=lax.Precision.HIGHEST)

def frame_update(obj_patch, probe_field, amplitude, forward, inverse):
    obj_re = obj_patch[:, 0, :].astype(jnp.float32)
    obj_im = obj_patch[:, 1, :].astype(jnp.float32)
    probe_re = probe_field[:, 0, :]
    probe_im = probe_field[:, 1, :]
    exit_wave = jnp.stack([probe_re * obj_re - probe_im * obj_im, probe_re * obj_im + probe_im * obj_re], axis=1).astype(jnp.bfloat16)
    far_field = transform(exit_wave, forward)
    modulus = jnp.sqrt(far_field[:, 0, :] ** 2 + far_field[:, 1, :] ** 2)
    factor = amplitude.astype(jnp.float32) / jnp.maximum(modulus, MODULUS_FLOOR) - 1.0
    change = (far_field * factor[:, None, :]).astype(jnp.bfloat16)
    back_field = transform(change, inverse)
    chi_re = back_field[:, 0, :]
    chi_im = back_field[:, 1, :]
    obj_step = jnp.stack([probe_re * chi_re + probe_im * chi_im, probe_re * chi_im - probe_im * chi_re], axis=1)
    grad_re = obj_re * chi_re + obj_im * chi_im
    grad_im = obj_re * chi_im - obj_im * chi_re
    weight = obj_re * obj_re + obj_im * obj_im
    return (obj_step, grad_re, grad_im, weight)

def reference(object_field, probe_field, amplitudes, row_offset, col_offset, counts):
    forward = dft_table(FRAME, 1.0)
    inverse = dft_table(FRAME, -1.0)
    object_half = lax.optimization_barrier(object_field.astype(jnp.bfloat16))
    slot_ids = jnp.arange(POSITIONS, dtype=jnp.int32)
    live_mask = (slot_ids % POS_DEV < counts[slot_ids // POS_DEV]).astype(jnp.float32)

    def scan_step(state_now, scan_item):
        update_sum, grad_re, grad_im, weight_sum = state_now
        amplitude, top_row, left_col, live_flag = scan_item
        start = (top_row.astype(jnp.int32), jnp.int32(0), left_col.astype(jnp.int32))
        obj_patch = lax.dynamic_slice(object_half, start, (FRAME, 2, FRAME))
        obj_step, part_re, part_im, weight = frame_update(obj_patch, probe_field, amplitude, forward, inverse)
        current = lax.dynamic_slice(update_sum, start, (FRAME, 2, FRAME))
        update_sum = lax.dynamic_update_slice(update_sum, current + live_flag * obj_step, start)
        return ((update_sum, grad_re + live_flag * part_re, grad_im + live_flag * part_im, weight_sum + live_flag * weight), None)
    zero_frame = jnp.zeros((FRAME, FRAME), jnp.float32)
    initial = (jnp.zeros(object_field.shape, jnp.float32), zero_frame, zero_frame, zero_frame)
    final_state, _ = lax.scan(scan_step, initial, (amplitudes, row_offset, col_offset, live_mask))
    update_sum, grad_re, grad_im, weight_sum = final_state
    probe_peak = jnp.max(probe_field[:, 0, :] ** 2 + probe_field[:, 1, :] ** 2) + EPSILON
    object_new = object_field + update_sum / probe_peak
    denominator = weight_sum + REGULARIZER
    probe_new = probe_field + jnp.stack([grad_re / denominator, grad_im / denominator], axis=1)
    return (object_new, probe_new)
```

```python
import functools
import math

import jax
import jax.numpy as jnp
import numpy as np
from jax import lax
from jax.experimental import pallas as pl
from jax.experimental.pallas import tpu as pltpu
from jax.sharding import PartitionSpec as P

FLOOR_SQUARED = 0.25
EPSILON = 1e-05
REGULARIZER = 1.0
F32 = jnp.float32
BF16 = jnp.bfloat16
MESH = pl.DeviceIdType.MESH
VMEM = pltpu.VMEM
LANES = 128
SHIFT = 64


def dft_tables(points):
    index = np.arange(points)
    product = (index[:, None] * index[None, :]) % points
    angle = (2.0 * math.pi / points) * product.astype(np.float32)
    norm = np.float32(1.0 / math.sqrt(points))
    cosine = (np.cos(angle.astype(np.float32)) * norm).astype(np.float32)
    sine = (np.sin(angle.astype(np.float32)) * norm).astype(np.float32)
    first = np.block([[cosine, sine], [-sine, cosine]])
    second = np.block([[cosine, -sine], [sine, cosine]])
    return jnp.asarray(first, BF16), jnp.asarray(second, BF16)


def greet(peers):
    barrier = pltpu.get_barrier_semaphore()
    expected = jnp.int32(0)
    for present, where in peers:
        expected = expected + present.astype(jnp.int32)

        @pl.when(present)
        def _(where=where):
            pl.semaphore_signal(barrier, inc=1, device_id=where, device_id_type=MESH)

    pl.semaphore_wait(barrier, expected)


def remote(src, dst, sems, slot, where):
    return pltpu.make_async_remote_copy(
        src_ref=src,
        dst_ref=dst,
        send_sem=sems.at[0, slot],
        recv_sem=sems.at[1, slot],
        device_id=where,
        device_id_type=MESH,
    )


def halo_kernel(rows_n, cols_n, obj_ref, ext_ref, sems):
    r = lax.axis_index("row")
    c = lax.axis_index("col")
    m = lax.axis_index("mode")
    _, tile_r, tile_c = obj_ref.shape
    half = tile_r // 2
    frame = ext_ref.shape[2] - tile_c
    has_up, has_down = r > 0, r < rows_n - 1
    has_left, has_right = c > 0, c < cols_n - 1
    sib = {"mode": 1 - m}
    up, down = {"row": r - 1}, {"row": r + 1}
    left, right = {"col": c - 1}, {"col": c + 1}
    always = m >= 0
    greet([(always, sib), (has_up, up), (has_down, down), (has_left, left), (has_right, right)])
    mine = pl.ds(pl.multiple_of(m * half, half), half)
    below = pl.ds(pl.multiple_of(tile_r + m * half, half), half)
    edge = pl.ds(tile_c, frame)
    body = pl.ds(0, tile_c)
    to_left = remote(obj_ref.at[:, mine, pl.ds(0, frame)], ext_ref.at[:, mine, edge], sems, 0, left)
    to_up = remote(obj_ref.at[:, mine, :], ext_ref.at[:, below, body], sems, 1, up)
    corner_up = remote(ext_ref.at[:, mine, edge], ext_ref.at[:, below, edge], sems, 2, up)
    swap_edge = remote(ext_ref.at[:, mine, edge], ext_ref.at[:, mine, edge], sems, 3, sib)
    swap_below = remote(ext_ref.at[:, below, body], ext_ref.at[:, below, body], sems, 4, sib)
    swap_corner = remote(ext_ref.at[:, below, edge], ext_ref.at[:, below, edge], sems, 5, sib)

    @pl.when(has_left)
    def _():
        to_left.start()

    @pl.when(has_up)
    def _():
        to_up.start()

    ext_ref[:, pl.ds(0, tile_r), body] = obj_ref[...]

    @pl.when(has_right)
    def _():
        to_left.wait_recv()

        @pl.when(has_up)
        def _():
            corner_up.start()

        swap_edge.start()

    @pl.when(has_down)
    def _():
        to_up.wait_recv()
        swap_below.start()

    @pl.when(has_right & has_down)
    def _():
        corner_up.wait_recv()
        swap_corner.start()
        swap_corner.wait()

    @pl.when(has_right)
    def _():
        swap_edge.wait()

        @pl.when(has_up)
        def _():
            corner_up.wait_send()

    @pl.when(has_down)
    def _():
        swap_below.wait()

    @pl.when(has_left)
    def _():
        to_left.wait_send()

    @pl.when(has_up)
    def _():
        to_up.wait_send()


def halo(obj, frame, rows_n, cols_n):
    planes, tile_r, tile_c = obj.shape
    return pl.pallas_call(
        functools.partial(halo_kernel, rows_n, cols_n),
        out_shape=jax.ShapeDtypeStruct((planes, tile_r + frame, tile_c + frame), BF16),
        in_specs=[pl.BlockSpec(memory_space=VMEM)],
        out_specs=pl.BlockSpec(memory_space=VMEM),
        scratch_shapes=[pltpu.SemaphoreType.DMA((2, 6))],
        compiler_params=pltpu.CompilerParams(
            collective_id=0, has_side_effects=True, vmem_limit_bytes=48 << 20
        ),
        name="halo",
    )(obj)


def frames_kernel(
    row_ref, col_ref, count_ref, ext_ref, probe_ref, amp_ref, first_ref, second_ref,
    upd_ref, sum_ref, obj, acc, tall, wide, field,
):
    frame = probe_ref.shape[1]
    ext_rows, ext_cols = ext_ref.shape[1:]
    top = lax.axis_index("row") * (ext_rows - frame)
    left = lax.axis_index("col") * (ext_cols - frame)
    step = 32
    for plane in range(2):
        for row in range(0, ext_rows, 64):
            rows = pl.ds(row, 64)
            value = ext_ref[plane, rows, :]
            obj[0, plane, rows, :] = value
            moved = pltpu.roll(value.astype(F32), ext_cols - SHIFT, 1)
            obj[1, plane, rows, :] = moved.astype(BF16)
    acc[...] = jnp.zeros_like(acc)
    sum_ref[...] = jnp.zeros_like(sum_ref)

    def one(slot, carry):
        row = row_ref[slot] - top
        col = col_ref[slot] - left
        odd = (col % LANES) // SHIFT
        cols = pl.ds(pl.multiple_of((col // LANES) * LANES, LANES), frame)
        for k in range(0, frame, step):
            rows = pl.ds(pl.multiple_of(row + k, step), step)
            o_re = obj[odd, 0, rows, cols].astype(F32)
            o_im = obj[odd, 1, rows, cols].astype(F32)
            p_re = probe_ref[0, k : k + step, :]
            p_im = probe_ref[1, k : k + step, :]
            tall[k : k + step, :] = (p_re * o_re - p_im * o_im).astype(BF16)
            tall[frame + k : frame + k + step, :] = (p_re * o_im + p_im * o_re).astype(BF16)
        half = jnp.dot(first_ref[...], tall[...], preferred_element_type=F32).astype(BF16)
        wide[:, :frame] = half[:frame]
        wide[:, frame:] = half[frame:]
        field[...] = jnp.dot(wide[...], second_ref[...], preferred_element_type=F32)
        for k in range(0, frame, step):
            f_re = field[k : k + step, :frame]
            f_im = field[k : k + step, frame:]
            amp = amp_ref[slot, k : k + step, :].astype(F32)
            power = f_re * f_re + f_im * f_im
            factor = amp * lax.rsqrt(jnp.maximum(power, FLOOR_SQUARED)) - 1.0
            tall[k : k + step, :] = (f_re * factor).astype(BF16)
            tall[frame + k : frame + k + step, :] = (f_im * factor).astype(BF16)
        half = jnp.dot(second_ref[...], tall[...], preferred_element_type=F32).astype(BF16)
        wide[:, :frame] = half[:frame]
        wide[:, frame:] = half[frame:]
        field[...] = jnp.dot(wide[...], first_ref[...], preferred_element_type=F32)
        for k in range(0, frame, step):
            rows = pl.ds(pl.multiple_of(row + k, step), step)
            here = pl.ds(k, step)
            x_re = field[k : k + step, :frame]
            x_im = field[k : k + step, frame:]
            o_re = obj[odd, 0, rows, cols].astype(F32)
            o_im = obj[odd, 1, rows, cols].astype(F32)
            p_re = probe_ref[0, k : k + step, :]
            p_im = probe_ref[1, k : k + step, :]
            acc[odd, 0, rows, cols] += p_re * x_re + p_im * x_im
            acc[odd, 1, rows, cols] += p_re * x_im - p_im * x_re
            sum_ref[0, here, :] += o_re * x_re + o_im * x_im
            sum_ref[1, here, :] += o_re * x_im - o_im * x_re
            sum_ref[2, here, :] += o_re * o_re + o_im * o_im
        return carry

    lax.fori_loop(0, count_ref[0], one, 0)
    for plane in range(2):
        for row in range(0, ext_rows, 64):
            rows = pl.ds(row, 64)
            upd_ref[plane, rows, :] = acc[0, plane, rows, :] + pltpu.roll(
                acc[1, plane, rows, :], SHIFT, 1
            )


def frames(row_offset, col_offset, counts, ext, probe, amplitudes, first, second):
    frame = probe.shape[1]
    in_vmem = pl.BlockSpec(memory_space=VMEM)
    in_smem = pl.BlockSpec(memory_space=pltpu.SMEM)
    return pl.pallas_call(
        frames_kernel,
        out_shape=(
            jax.ShapeDtypeStruct(ext.shape, F32),
            jax.ShapeDtypeStruct((3, frame, frame), F32),
        ),
        in_specs=[in_smem] * 3 + [in_vmem] * 5,
        out_specs=(in_vmem, in_vmem),
        scratch_shapes=[
            VMEM((2, *ext.shape), BF16),
            VMEM((2, *ext.shape), F32),
            VMEM((2 * frame, frame), BF16),
            VMEM((frame, 2 * frame), BF16),
            VMEM((frame, 2 * frame), F32),
        ],
        compiler_params=pltpu.CompilerParams(vmem_limit_bytes=48 << 20),
        name="frames",
    )(row_offset, col_offset, counts, ext, probe, amplitudes, first, second)


def merge_kernel(
    rows_n, cols_n, with_probe, upd_ref, sum_ref, probe_ref, share_ref, fresh_ref,
    total, got, from_left, from_up, got_sum, part, col_got, row_part, row_got, sems, psems,
):
    r = lax.axis_index("row")
    c = lax.axis_index("col")
    m = lax.axis_index("mode")
    half, tile_c = share_ref.shape[1:]
    tile_r = 2 * half
    frame = probe_ref.shape[1]
    has_up, has_down = r > 0, r < rows_n - 1
    has_left, has_right = c > 0, c < cols_n - 1
    sib = {"mode": 1 - m}
    up, down = {"row": r - 1}, {"row": r + 1}
    left, right = {"col": c - 1}, {"col": c + 1}
    always = m >= 0
    row_peers = [{"row": lax.rem(r + d, rows_n)} for d in range(1, rows_n)]
    col_peers = [{"col": lax.rem(c + d, cols_n)} for d in range(1, cols_n)]
    if with_probe:
        greet([(always, p) for p in [sib] + row_peers + col_peers])
    else:
        greet([(always, sib), (has_up, up), (has_down, down), (has_left, left), (has_right, right)])

    def block(which, base):
        return pl.ds(pl.multiple_of(which * half + base, half), half)

    top_mine, low_mine = block(m, 0), block(m, tile_r)
    top_sib, low_sib = block(1 - m, 0), block(1 - m, tile_r)
    first_cols, mid_cols, edge = pl.ds(0, frame), pl.ds(frame, tile_c - frame), pl.ds(tile_c, frame)
    pieces = [(1, edge), (1, mid_cols), (0, edge), (1, first_cols), (0, pl.ds(0, tile_c))]
    if with_probe:
        sum_rows = frame // 2
        col_rows = sum_rows // cols_n
        row_rows = col_rows // rows_n
        mine_at = m * sum_rows
        give = sum_ref.at[:, pl.ds(pl.multiple_of((1 - m) * sum_rows, sum_rows), sum_rows), :]
        swap_sum = remote(give, got_sum, psems, 0, sib)
        swap_sum.start()
    swaps = []
    for slot, (low, cols) in enumerate(pieces):
        src = upd_ref.at[:, low_sib if low else top_sib, cols]
        swaps.append(remote(src, got.at[low, :, :, cols], sems, slot, sib))
        swaps[-1].start()

    def joined(index):
        low, cols = pieces[index]
        swaps[index].wait_recv()
        total[low, :, :, cols] = upd_ref[:, low_mine if low else top_mine, cols] + got[low, :, :, cols]

    corner = remote(total.at[1, :, :, edge], from_left.at[1], sems, 5, right)
    side = remote(total.at[0, :, :, edge], from_left.at[0], sems, 6, right)
    fall_mid = remote(total.at[1, :, :, mid_cols], from_up.at[:, :, mid_cols], sems, 7, down)
    fall_first = remote(total.at[1, :, :, first_cols], from_up.at[:, :, first_cols], sems, 8, down)

    if with_probe:
        swap_sum.wait_recv()
        at = pl.ds(pl.multiple_of(mine_at, sum_rows), sum_rows)
        part[...] = sum_ref[:, at, :] + got_sum[...]
        col_copies = []
        for d in range(1, cols_n):
            there = lax.rem(c + d, cols_n)
            src = part.at[:, pl.ds(pl.multiple_of(there * col_rows, col_rows), col_rows), :]
            col_copies.append(remote(src, col_got.at[d - 1], psems, d, col_peers[d - 1]))
            col_copies[-1].start()
    joined(0)

    @pl.when(has_right)
    def _():
        corner.start()

    joined(1)

    @pl.when(has_down)
    def _():
        fall_mid.start()

    joined(2)

    @pl.when(has_right)
    def _():
        side.start()

    joined(3)
    base = cols_n
    if with_probe:
        own = part[:, pl.ds(pl.multiple_of(c * col_rows, col_rows), col_rows), :]
        for d in range(1, cols_n):
            col_copies[d - 1].wait_recv()
            own = own + col_got[d - 1]
        row_part[...] = own
        row_copies = []
        for d in range(1, rows_n):
            there = lax.rem(r + d, rows_n)
            src = row_part.at[:, pl.ds(pl.multiple_of(there * row_rows, row_rows), row_rows), :]
            row_copies.append(remote(src, row_got.at[d - 1], psems, base + d, row_peers[d - 1]))
            row_copies[-1].start()

    @pl.when(has_left)
    def _():
        corner.wait_recv()
        total[1, :, :, first_cols] += from_left[1]

    @pl.when(has_down)
    def _():
        fall_first.start()

    peak = probe_ref[0] * probe_ref[0] + probe_ref[1] * probe_ref[1]
    peak = jnp.max(peak, keepdims=True) + EPSILON
    base += rows_n
    if with_probe:
        own = row_part[:, pl.ds(pl.multiple_of(r * row_rows, row_rows), row_rows), :]
        for d in range(1, rows_n):
            row_copies[d - 1].wait_recv()
            own = own + row_got[d - 1]
        weight = own[2] + REGULARIZER
        start = mine_at + c * col_rows
        shard = pl.ds(pl.multiple_of(start + r * row_rows, row_rows), row_rows)
        fresh_ref[0, shard, :] = probe_ref[0, shard, :] + own[0] / weight
        fresh_ref[1, shard, :] = probe_ref[1, shard, :] + own[1] / weight
        spread = []
        for d in range(1, rows_n):
            ref = fresh_ref.at[:, shard, :]
            spread.append(remote(ref, ref, psems, base + d, row_peers[d - 1]))
            spread[-1].start()
        base += rows_n
        for d in range(1, rows_n):
            spread[d - 1].wait_recv()
        ref = fresh_ref.at[:, pl.ds(pl.multiple_of(start, col_rows), col_rows), :]
        for d in range(1, cols_n):
            spread.append(remote(ref, ref, psems, base + d, col_peers[d - 1]))
            spread[-1].start()
        base += cols_n
    else:
        fresh_ref[...] = jnp.zeros_like(fresh_ref)
    joined(4)

    @pl.when(has_left)
    def _():
        side.wait_recv()
        total[0, :, :, first_cols] += from_left[0]

    if with_probe:
        for d in range(1, cols_n):
            spread[rows_n - 1 + d - 1].wait_recv()
        ref = fresh_ref.at[:, pl.ds(pl.multiple_of(mine_at, sum_rows), sum_rows), :]
        last = remote(ref, ref, psems, base, sib)
        last.start()

    @pl.when(has_up)
    def _():
        fall_mid.wait_recv()
        fall_first.wait_recv()
        total[0, :, :, pl.ds(0, tile_c)] += from_up[...]

    share_ref[...] = total[0, :, :, pl.ds(0, tile_c)] / peak

    for copy in swaps:
        copy.wait_send()

    @pl.when(has_right)
    def _():
        corner.wait_send()
        side.wait_send()

    @pl.when(has_down)
    def _():
        fall_mid.wait_send()
        fall_first.wait_send()

    if with_probe:
        swap_sum.wait_send()
        for copy in col_copies + row_copies + spread:
            copy.wait_send()
        last.wait()


def merge(upd, sums, probe, tile_r, tile_c, rows_n, cols_n, with_probe):
    frame = probe.shape[1]
    half = tile_r // 2
    ext_c = tile_c + frame
    sum_rows = frame // 2
    if with_probe:
        col_rows = sum_rows // cols_n
        row_rows = col_rows // rows_n
    else:
        col_rows = row_rows = 8
    in_vmem = pl.BlockSpec(memory_space=VMEM)
    return pl.pallas_call(
        functools.partial(merge_kernel, rows_n, cols_n, with_probe),
        out_shape=(
            jax.ShapeDtypeStruct((2, half, tile_c), F32),
            jax.ShapeDtypeStruct((2, frame, frame), F32),
        ),
        in_specs=[in_vmem] * 3,
        out_specs=(in_vmem, in_vmem),
        scratch_shapes=[
            VMEM((2, 2, half, ext_c), F32),
            VMEM((2, 2, half, ext_c), F32),
            VMEM((2, 2, half, frame), F32),
            VMEM((2, half, tile_c), F32),
            VMEM((3, sum_rows, frame), F32),
            VMEM((3, sum_rows, frame), F32),
            VMEM((max(1, cols_n - 1), 3, col_rows, frame), F32),
            VMEM((3, col_rows, frame), F32),
            VMEM((max(1, rows_n - 1), 3, row_rows, frame), F32),
            pltpu.SemaphoreType.DMA((2, 9)),
            pltpu.SemaphoreType.DMA((2, 2 * rows_n + 2 * cols_n + 1)),
        ],
        compiler_params=pltpu.CompilerParams(
            collective_id=1, has_side_effects=True, vmem_limit_bytes=48 << 20
        ),
        name="merge",
    )(upd, sums, probe)


def body(rows_n, cols_n, object_field, probe_field, amplitudes, row_offset, col_offset, counts):
    tile_r, _, tile_c = object_field.shape
    frame = probe_field.shape[0]
    half = tile_r // 2
    first, second = dft_tables(frame)
    obj = jnp.moveaxis(object_field.astype(BF16), 1, 0)
    probe = jnp.moveaxis(probe_field, 1, 0)
    ext = halo(obj, frame, rows_n, cols_n)
    upd, sums = frames(row_offset, col_offset, counts, ext, probe, amplitudes, first, second)
    with_probe = frame % (2 * rows_n * cols_n * 8) == 0
    share, fresh = merge(upd, sums, probe, tile_r, tile_c, rows_n, cols_n, with_probe)
    rows_here = lax.dynamic_slice_in_dim(object_field, lax.axis_index("mode") * half, half, 0)
    object_new = rows_here + jnp.moveaxis(share, 0, 1)
    if with_probe:
        return (object_new, jnp.moveaxis(fresh, 0, 1))
    sums = lax.psum(sums, ("row", "col", "mode"))
    fresh = probe + sums[:2] / (sums[2:] + REGULARIZER)
    return (object_new, jnp.moveaxis(fresh, 0, 1))


def solution(mesh):
    split = ("groups", "row", "col", "mode")
    placed = (
        P(("groups", "row"), None, "col"),
        P("groups", None, None),
        P(split, None, None),
        P(split),
        P(split),
        P(split),
    )
    return jax.shard_map(
        functools.partial(body, mesh.shape["row"], mesh.shape["col"]),
        mesh=mesh,
        in_specs=placed,
        out_specs=(P(("groups", "row", "mode"), None, "col"), P("groups", None, None)),
        check_vma=False,
    )
```

```python
import functools
import math

import jax
import jax.numpy as jnp
import numpy as np
from jax import lax
from jax.experimental import pallas as pl
from jax.experimental.pallas import tpu as pltpu
from jax.sharding import PartitionSpec as P

FLOOR_SQUARED = 0.25
EPSILON = 1e-05
REGULARIZER = 1.0
F32 = jnp.float32
BF16 = jnp.bfloat16
MESH = pl.DeviceIdType.MESH
VMEM = pltpu.VMEM
LANES = 128
SHIFT = 64


def dft_tables(points):
    index = np.arange(points)
    product = (index[:, None] * index[None, :]) % points
    angle = (2.0 * math.pi / points) * product.astype(np.float32)
    norm = np.float32(1.0 / math.sqrt(points))
    cosine = (np.cos(angle.astype(np.float32)) * norm).astype(np.float32)
    sine = (np.sin(angle.astype(np.float32)) * norm).astype(np.float32)
    first = np.block([[cosine, sine], [-sine, cosine]])
    second = np.block([[cosine, -sine], [sine, cosine]])
    return jnp.asarray(first, BF16), jnp.asarray(second, BF16)


def greet(peers):
    barrier = pltpu.get_barrier_semaphore()
    expected = jnp.int32(0)
    for present, where in peers:
        expected = expected + present.astype(jnp.int32)

        @pl.when(present)
        def _(where=where):
            pl.semaphore_signal(barrier, inc=1, device_id=where, device_id_type=MESH)

    pl.semaphore_wait(barrier, expected)


def remote(src, dst, sems, slot, where):
    return pltpu.make_async_remote_copy(
        src_ref=src,
        dst_ref=dst,
        send_sem=sems.at[0, slot],
        recv_sem=sems.at[1, slot],
        device_id=where,
        device_id_type=MESH,
    )


def halo_kernel(rows_n, cols_n, field_ref, probe_ref, obj_ref, planes_ref, acc_ref, sems):
    r = lax.axis_index("row")
    c = lax.axis_index("col")
    m = lax.axis_index("mode")
    tile_r, _, tile_c = field_ref.shape
    frame = probe_ref.shape[0]
    half, reach = tile_r // 2, frame - SHIFT
    low = reach // 2
    has_up, has_down = r > 0, r < rows_n - 1
    has_left, has_right = c > 0, c < cols_n - 1
    sib = {"mode": 1 - m}
    up, down = {"row": r - 1}, {"row": r + 1}
    left, right = {"col": c - 1}, {"col": c + 1}
    always = m >= 0
    greet([(always, sib), (has_up, up), (has_down, down), (has_left, left), (has_right, right)])
    ext = obj_ref.at[0]
    mine = pl.ds(pl.multiple_of(m * half, half), half)
    other = pl.ds(pl.multiple_of((1 - m) * half, half), half)
    lift = pl.ds(pl.multiple_of(m * low, 32), low)
    below = pl.ds(pl.multiple_of(tile_r + m * low, 32), low)
    edge = pl.ds(tile_c, frame)
    body = pl.ds(0, tile_c)
    to_left = remote(ext.at[:, mine, pl.ds(0, frame)], ext.at[:, mine, edge], sems, 0, left)
    to_up = remote(ext.at[:, lift, body], ext.at[:, below, body], sems, 1, up)
    swap_edge = remote(ext.at[:, mine, edge], ext.at[:, mine, edge], sems, 2, sib)
    corner_up = remote(ext.at[:, lift, edge], ext.at[:, below, edge], sems, 3, up)
    swap_below = remote(ext.at[:, below, body], ext.at[:, below, body], sems, 4, sib)
    swap_corner = remote(ext.at[:, below, edge], ext.at[:, below, edge], sems, 5, sib)

    def convert(rows):
        for plane in range(2):
            obj_ref[0, plane, rows, body] = field_ref[rows, plane, :].astype(BF16)

    def shifted(rows, start, width):
        for plane in range(2):
            value = obj_ref[0, plane, rows, pl.ds(start, width + LANES)].astype(F32)
            value = pltpu.roll(value, width + LANES - SHIFT, 1)[:, :width]
            obj_ref[1, plane, rows, pl.ds(start, width)] = value.astype(BF16)

    convert(mine)

    @pl.when(has_left)
    def _():
        to_left.start()

    convert(other)

    @pl.when(has_up)
    def _():
        to_up.start()

    for plane in range(2):
        planes_ref[plane] = probe_ref[:, plane, :]
    top, bottom = pl.ds(0, tile_r), pl.ds(tile_r, reach)
    shifted(top, 0, tile_c - LANES)
    acc_ref[0] = jnp.zeros(acc_ref.shape[1:], F32)

    @pl.when(has_right)
    def _():
        to_left.wait_recv()
        swap_edge.start()

    acc_ref[1] = jnp.zeros(acc_ref.shape[1:], F32)

    @pl.when(has_right)
    def _():
        swap_edge.wait_recv()

        @pl.when(has_up)
        def _():
            corner_up.start()

        shifted(top, tile_c - LANES, frame)

    @pl.when(has_down)
    def _():
        to_up.wait_recv()
        swap_below.start()
        swap_below.wait_recv()
        shifted(bottom, 0, tile_c - LANES)

    @pl.when(has_right & has_down)
    def _():
        corner_up.wait_recv()
        swap_corner.start()
        swap_corner.wait()
        shifted(bottom, tile_c - LANES, frame)

    @pl.when(has_right)
    def _():
        swap_edge.wait_send()

        @pl.when(has_up)
        def _():
            corner_up.wait_send()

    @pl.when(has_down)
    def _():
        swap_below.wait_send()

    @pl.when(has_left)
    def _():
        to_left.wait_send()

    @pl.when(has_up)
    def _():
        to_up.wait_send()


def halo(field, probe, rows_n, cols_n):
    tile_r, planes, tile_c = field.shape
    frame = probe.shape[0]
    shape = (2, planes, tile_r + frame, tile_c + frame)
    in_vmem = pl.BlockSpec(memory_space=VMEM)
    return pl.pallas_call(
        functools.partial(halo_kernel, rows_n, cols_n),
        out_shape=(
            jax.ShapeDtypeStruct(shape, BF16),
            jax.ShapeDtypeStruct((planes, frame, frame), F32),
            jax.ShapeDtypeStruct(shape, F32),
        ),
        in_specs=[in_vmem] * 2,
        out_specs=(in_vmem,) * 3,
        scratch_shapes=[pltpu.SemaphoreType.DMA((2, 6))],
        cost_estimate=pl.CostEstimate(flops=0, bytes_accessed=40 << 20, transcendentals=0),
        compiler_params=pltpu.CompilerParams(
            collective_id=0, has_side_effects=True, vmem_limit_bytes=4 << 20
        ),
        name="halo",
    )(field, probe)


def frames_kernel(
    row_ref, col_ref, count_ref, obj, probe_ref, amp_ref, first_ref, second_ref, _zero,
    acc, sum_ref, tall, wide, field,
):
    frame = probe_ref.shape[1]
    ext_rows, ext_cols = obj.shape[2:]
    top = lax.axis_index("row") * (ext_rows - frame)
    left = lax.axis_index("col") * (ext_cols - frame)
    step = 32
    sum_ref[...] = jnp.zeros_like(sum_ref)

    def one(slot, carry):
        row = row_ref[slot] - top
        col = col_ref[slot] - left
        odd = (col % LANES) // SHIFT
        cols = pl.ds(pl.multiple_of((col // LANES) * LANES, LANES), frame)
        for k in range(0, frame, step):
            rows = pl.ds(pl.multiple_of(row + k, step), step)
            o_re = obj[odd, 0, rows, cols].astype(F32)
            o_im = obj[odd, 1, rows, cols].astype(F32)
            p_re = probe_ref[0, k : k + step, :]
            p_im = probe_ref[1, k : k + step, :]
            tall[k : k + step, :] = (p_re * o_re - p_im * o_im).astype(BF16)
            tall[frame + k : frame + k + step, :] = (p_re * o_im + p_im * o_re).astype(BF16)
        half = jnp.dot(first_ref[...], tall[...], preferred_element_type=F32).astype(BF16)
        wide[:, :frame] = half[:frame]
        wide[:, frame:] = half[frame:]
        field[...] = jnp.dot(wide[...], second_ref[...], preferred_element_type=F32)
        for k in range(0, frame, step):
            f_re = field[k : k + step, :frame]
            f_im = field[k : k + step, frame:]
            amp = amp_ref[slot, k : k + step, :].astype(F32)
            power = f_re * f_re + f_im * f_im
            factor = amp * lax.rsqrt(jnp.maximum(power, FLOOR_SQUARED)) - 1.0
            tall[k : k + step, :] = (f_re * factor).astype(BF16)
            tall[frame + k : frame + k + step, :] = (f_im * factor).astype(BF16)
        half = jnp.dot(second_ref[...], tall[...], preferred_element_type=F32).astype(BF16)
        wide[:, :frame] = half[:frame]
        wide[:, frame:] = half[frame:]
        field[...] = jnp.dot(wide[...], first_ref[...], preferred_element_type=F32)
        for k in range(0, frame, step):
            rows = pl.ds(pl.multiple_of(row + k, step), step)
            here = pl.ds(k, step)
            x_re = field[k : k + step, :frame]
            x_im = field[k : k + step, frame:]
            o_re = obj[odd, 0, rows, cols].astype(F32)
            o_im = obj[odd, 1, rows, cols].astype(F32)
            p_re = probe_ref[0, k : k + step, :]
            p_im = probe_ref[1, k : k + step, :]
            acc[odd, 0, rows, cols] += p_re * x_re + p_im * x_im
            acc[odd, 1, rows, cols] += p_re * x_im - p_im * x_re
            sum_ref[0, here, :] += o_re * x_re + o_im * x_im
            sum_ref[1, here, :] += o_re * x_im - o_im * x_re
            sum_ref[2, here, :] += o_re * o_re + o_im * o_im
        return carry

    lax.fori_loop(0, count_ref[0], one, 0)
    for plane in range(2):
        for row in range(0, ext_rows - SHIFT, SHIFT):
            rows = pl.ds(row, SHIFT)
            acc[0, plane, rows, :] += pltpu.roll(acc[1, plane, rows, :], SHIFT, 1)


def frames(row_offset, col_offset, counts, obj, probe, amplitudes, first, second, acc):
    frame = probe.shape[1]
    in_vmem = pl.BlockSpec(memory_space=VMEM)
    in_smem = pl.BlockSpec(memory_space=pltpu.SMEM)
    return pl.pallas_call(
        frames_kernel,
        out_shape=(
            jax.ShapeDtypeStruct(acc.shape, F32),
            jax.ShapeDtypeStruct((3, frame, frame), F32),
        ),
        in_specs=[in_smem] * 3 + [in_vmem] * 6,
        out_specs=(in_vmem, in_vmem),
        input_output_aliases={8: 0},
        scratch_shapes=[
            VMEM((2 * frame, frame), BF16),
            VMEM((frame, 2 * frame), BF16),
            VMEM((frame, 2 * frame), F32),
        ],
        compiler_params=pltpu.CompilerParams(vmem_limit_bytes=10 << 20),
        name="frames",
    )(row_offset, col_offset, counts, obj, probe, amplitudes, first, second, acc)


def merge_kernel(
    rows_n, cols_n, with_probe, acc_ref, sum_ref, probe_ref, field_ref, share_ref, out_ref,
    fresh_ref, got, total, low_first, to_right, to_down, from_left, from_up,
    got_sum, part, col_got, row_part, row_got, sems, psems,
):
    r = lax.axis_index("row")
    c = lax.axis_index("col")
    m = lax.axis_index("mode")
    half, _, tile_c = share_ref.shape
    tile_r = 2 * half
    frame = probe_ref.shape[1]
    upd_ref = acc_ref.at[0]
    has_up, has_down = r > 0, r < rows_n - 1
    has_left, has_right = c > 0, c < cols_n - 1
    sib = {"mode": 1 - m}
    up, down = {"row": r - 1}, {"row": r + 1}
    left, right = {"col": c - 1}, {"col": c + 1}
    always = m >= 0
    row_peers = [{"row": lax.rem(r + d, rows_n)} for d in range(1, rows_n)]
    col_peers = [{"col": lax.rem(c + d, cols_n)} for d in range(1, cols_n)]
    if with_probe:
        greet([(always, p) for p in [sib] + row_peers + col_peers])
    else:
        greet([(always, sib), (has_up, up), (has_down, down), (has_left, left), (has_right, right)])

    def block(which, base):
        return pl.ds(pl.multiple_of(which * half + base, half), half)

    top_mine, low_mine = block(m, 0), block(m, tile_r)
    top_sib, low_sib = block(1 - m, 0), block(1 - m, tile_r)
    first_cols, mid_cols, edge = pl.ds(0, frame), pl.ds(frame, tile_c - frame), pl.ds(tile_c, frame)
    pieces = [(1, edge), (1, mid_cols), (0, edge), (1, first_cols), (0, pl.ds(0, tile_c))]
    if with_probe:
        sum_rows = frame // 2
        col_rows = sum_rows // cols_n
        row_rows = col_rows // rows_n
        mine_at = m * sum_rows
        give = sum_ref.at[:, pl.ds(pl.multiple_of((1 - m) * sum_rows, sum_rows), sum_rows), :]
        swap_sum = remote(give, got_sum, psems, 0, sib)
        swap_sum.start()
    swaps = []
    for slot, (low, cols) in enumerate(pieces):
        src = upd_ref.at[:, low_sib if low else top_sib, cols]
        swaps.append(remote(src, got.at[low, :, :, cols], sems, slot, sib))
        swaps[-1].start()

    def joined(index):
        low, cols = pieces[index]
        swaps[index].wait_recv()
        return upd_ref[:, low_mine if low else top_mine, cols] + got[low, :, :, cols]

    corner = remote(to_right.at[1], from_left.at[1], sems, 5, right)
    side = remote(to_right.at[0], from_left.at[0], sems, 6, right)
    fall_mid = remote(to_down.at[:, :, mid_cols], from_up.at[:, :, mid_cols], sems, 7, down)
    fall_first = remote(to_down.at[:, :, first_cols], from_up.at[:, :, first_cols], sems, 8, down)

    if with_probe:
        swap_sum.wait_recv()
        at = pl.ds(pl.multiple_of(mine_at, sum_rows), sum_rows)
        part[...] = sum_ref[:, at, :] + got_sum[...]
        col_copies = []
        for d in range(1, cols_n):
            there = lax.rem(c + d, cols_n)
            src = part.at[:, pl.ds(pl.multiple_of(there * col_rows, col_rows), col_rows), :]
            col_copies.append(remote(src, col_got.at[d - 1], psems, d, col_peers[d - 1]))
            col_copies[-1].start()
    to_right[1] = joined(0).astype(BF16)

    @pl.when(has_right)
    def _():
        corner.start()

    to_down[:, :, mid_cols] = joined(1).astype(BF16)

    @pl.when(has_down)
    def _():
        fall_mid.start()

    to_right[0] = joined(2).astype(BF16)

    @pl.when(has_right)
    def _():
        side.start()

    low_first[...] = joined(3)
    base = cols_n
    if with_probe:
        own = part[:, pl.ds(pl.multiple_of(c * col_rows, col_rows), col_rows), :]
        for d in range(1, cols_n):
            col_copies[d - 1].wait_recv()
            own = own + col_got[d - 1]
        row_part[...] = own
        row_copies = []
        for d in range(1, rows_n):
            there = lax.rem(r + d, rows_n)
            src = row_part.at[:, pl.ds(pl.multiple_of(there * row_rows, row_rows), row_rows), :]
            row_copies.append(remote(src, row_got.at[d - 1], psems, base + d, row_peers[d - 1]))
            row_copies[-1].start()

    @pl.when(has_left)
    def _():
        corner.wait_recv()
        low_first[...] += from_left[1].astype(F32)

    @pl.when(has_down)
    def _():
        to_down[:, :, first_cols] = low_first[...].astype(BF16)
        fall_first.start()

    peak = probe_ref[0] * probe_ref[0] + probe_ref[1] * probe_ref[1]
    peak = jnp.max(peak, keepdims=True) + EPSILON
    base += rows_n
    if with_probe:
        own = row_part[:, pl.ds(pl.multiple_of(r * row_rows, row_rows), row_rows), :]
        for d in range(1, rows_n):
            row_copies[d - 1].wait_recv()
            own = own + row_got[d - 1]
        weight = own[2] + REGULARIZER
        start = mine_at + c * col_rows
        shard = pl.ds(pl.multiple_of(start + r * row_rows, row_rows), row_rows)
        fresh_ref[0, shard, :] = probe_ref[0, shard, :] + own[0] / weight
        fresh_ref[1, shard, :] = probe_ref[1, shard, :] + own[1] / weight
        spread = []
        for d in range(1, rows_n):
            ref = fresh_ref.at[:, shard, :]
            spread.append(remote(ref, ref, psems, base + d, row_peers[d - 1]))
            spread[-1].start()
        base += rows_n
        for d in range(1, rows_n):
            spread[d - 1].wait_recv()
        ref = fresh_ref.at[:, pl.ds(pl.multiple_of(start, col_rows), col_rows), :]
        for d in range(1, cols_n):
            spread.append(remote(ref, ref, psems, base + d, col_peers[d - 1]))
            spread[-1].start()
        base += cols_n
    else:
        fresh_ref[...] = jnp.zeros_like(fresh_ref)
    total[...] = joined(4)

    @pl.when(has_left)
    def _():
        side.wait_recv()
        total[:, :, first_cols] += from_left[0].astype(F32)

    if with_probe:
        for d in range(1, cols_n):
            spread[rows_n - 1 + d - 1].wait_recv()
        ref = fresh_ref.at[:, pl.ds(pl.multiple_of(mine_at, sum_rows), sum_rows), :]
        last = remote(ref, ref, psems, base, sib)
        last.start()

    @pl.when(has_up)
    def _():
        fall_mid.wait_recv()
        fall_first.wait_recv()
        total[...] += from_up[...].astype(F32)

    for plane in range(2):
        share_ref[:, plane, :] = field_ref[top_mine, plane, :] + total[plane] / peak

    for copy in swaps:
        copy.wait_send()

    @pl.when(has_right)
    def _():
        corner.wait_send()
        side.wait_send()

    @pl.when(has_down)
    def _():
        fall_mid.wait_send()
        fall_first.wait_send()

    if with_probe:
        swap_sum.wait_send()
        for copy in col_copies + row_copies + spread:
            copy.wait_send()
        last.wait()
    for plane in range(2):
        out_ref[:, plane, :] = fresh_ref[plane]


def merge(acc, sums, probe, field, rows_n, cols_n, with_probe):
    tile_r, _, tile_c = field.shape
    frame = probe.shape[1]
    half = tile_r // 2
    ext_c = tile_c + frame
    sum_rows = frame // 2
    if with_probe:
        col_rows = sum_rows // cols_n
        row_rows = col_rows // rows_n
    else:
        col_rows = row_rows = 8
    in_vmem = pl.BlockSpec(memory_space=VMEM)
    return pl.pallas_call(
        functools.partial(merge_kernel, rows_n, cols_n, with_probe),
        out_shape=(
            jax.ShapeDtypeStruct((half, 2, tile_c), F32),
            jax.ShapeDtypeStruct((frame, 2, frame), F32),
        ),
        in_specs=[in_vmem] * 4,
        out_specs=(in_vmem, in_vmem),
        scratch_shapes=[
            VMEM((2, frame, frame), F32),
            VMEM((2, 2, half, ext_c), F32),
            VMEM((2, half, tile_c), F32),
            VMEM((2, half, frame), F32),
            VMEM((2, 2, half, frame), BF16),
            VMEM((2, half, tile_c), BF16),
            VMEM((2, 2, half, frame), BF16),
            VMEM((2, half, tile_c), BF16),
            VMEM((3, sum_rows, frame), F32),
            VMEM((3, sum_rows, frame), F32),
            VMEM((max(1, cols_n - 1), 3, col_rows, frame), F32),
            VMEM((3, col_rows, frame), F32),
            VMEM((max(1, rows_n - 1), 3, row_rows, frame), F32),
            pltpu.SemaphoreType.DMA((2, 9)),
            pltpu.SemaphoreType.DMA((2, 2 * rows_n + 2 * cols_n + 1)),
        ],
        compiler_params=pltpu.CompilerParams(
            collective_id=1, has_side_effects=True, vmem_limit_bytes=14 << 20
        ),
        name="merge",
    )(acc, sums, probe, field)


def body(rows_n, cols_n, object_field, probe_field, amplitudes, row_offset, col_offset, counts):
    frame = probe_field.shape[0]
    first, second = dft_tables(frame)
    obj, probe, acc = halo(object_field, probe_field, rows_n, cols_n)
    acc, sums = frames(
        row_offset, col_offset, counts, obj, probe, amplitudes, first, second, acc
    )
    with_probe = frame % (2 * rows_n * cols_n * 8) == 0
    object_new, fresh = merge(acc, sums, probe, object_field, rows_n, cols_n, with_probe)
    if not with_probe:
        sums = lax.psum(sums, ("row", "col", "mode"))
        fresh = probe + sums[:2] / (sums[2:] + REGULARIZER)
        fresh = jnp.moveaxis(fresh, 0, 1)
    return (object_new, fresh)


def solution(mesh):
    split = ("groups", "row", "col", "mode")
    placed = (
        P(("groups", "row"), None, "col"),
        P("groups", None, None),
        P(split, None, None),
        P(split),
        P(split),
        P(split),
    )
    return jax.shard_map(
        functools.partial(body, mesh.shape["row"], mesh.shape["col"]),
        mesh=mesh,
        in_specs=placed,
        out_specs=(P(("groups", "row", "mode"), None, "col"), P("groups", None, None)),
        check_vma=False,
    )
```

```python
import functools
import math

import jax
import jax.numpy as jnp
import numpy as np
from jax import lax
from jax.experimental import pallas as pl
from jax.experimental.pallas import tpu as pltpu
from jax.sharding import PartitionSpec as P

FLOOR_SQUARED = 0.25
EPSILON = 1e-05
REGULARIZER = 1.0
F32 = jnp.float32
BF16 = jnp.bfloat16
MESH = pl.DeviceIdType.MESH
VMEM = pltpu.VMEM
LANES = 128
SHIFT = 64


def dft_tables(points):
    index = np.arange(points)
    product = (index[:, None] * index[None, :]) % points
    angle = (2.0 * math.pi / points) * product.astype(np.float32)
    norm = np.float32(1.0 / math.sqrt(points))
    cosine = (np.cos(angle.astype(np.float32)) * norm).astype(np.float32)
    sine = (np.sin(angle.astype(np.float32)) * norm).astype(np.float32)
    first = np.block([[cosine, sine], [-sine, cosine]])
    second = np.block([[cosine, -sine], [sine, cosine]])
    return jnp.asarray(first, BF16), jnp.asarray(second, BF16)


def greet(peers):
    barrier = pltpu.get_barrier_semaphore()
    expected = jnp.int32(0)
    for present, where in peers:
        expected = expected + present.astype(jnp.int32)

        @pl.when(present)
        def _(where=where):
            pl.semaphore_signal(barrier, inc=1, device_id=where, device_id_type=MESH)

    pl.semaphore_wait(barrier, expected)


def remote(src, dst, sems, slot, where):
    return pltpu.make_async_remote_copy(
        src_ref=src,
        dst_ref=dst,
        send_sem=sems.at[0, slot],
        recv_sem=sems.at[1, slot],
        device_id=where,
        device_id_type=MESH,
    )


def halo_kernel(rows_n, cols_n, count, *refs):
    field_hbm, probe_hbm = refs[:2]
    extras = refs[2 : 2 + count]
    obj_ref, planes_ref, acc_ref = refs[2 + count : 5 + count]
    landed = refs[5 + count : 5 + 2 * count]
    field_ref, probe_ref, sems, local = refs[5 + 2 * count :]
    pairs = [(field_hbm, field_ref), (probe_hbm, probe_ref), *zip(extras, landed)]
    fetches = [pltpu.make_async_copy(a, b, local.at[i]) for i, (a, b) in enumerate(pairs)]
    for fetch in fetches:
        fetch.start()
    r = lax.axis_index("row")
    c = lax.axis_index("col")
    m = lax.axis_index("mode")
    tile_r, _, tile_c = field_ref.shape
    frame = probe_ref.shape[0]
    half, reach = tile_r // 2, frame - SHIFT
    low = reach // 2
    has_up, has_down = r > 0, r < rows_n - 1
    has_left, has_right = c > 0, c < cols_n - 1
    sib = {"mode": 1 - m}
    up, down = {"row": r - 1}, {"row": r + 1}
    left, right = {"col": c - 1}, {"col": c + 1}
    always = m >= 0
    greet([(always, sib), (has_up, up), (has_down, down), (has_left, left), (has_right, right)])
    ext = obj_ref.at[0]
    mine = pl.ds(pl.multiple_of(m * half, half), half)
    other = pl.ds(pl.multiple_of((1 - m) * half, half), half)
    lift = pl.ds(pl.multiple_of(m * low, 32), low)
    below = pl.ds(pl.multiple_of(tile_r + m * low, 32), low)
    edge = pl.ds(tile_c, frame)
    body = pl.ds(0, tile_c)
    to_left = remote(ext.at[:, mine, pl.ds(0, frame)], ext.at[:, mine, edge], sems, 0, left)
    to_up = remote(ext.at[:, lift, body], ext.at[:, below, body], sems, 1, up)
    swap_edge = remote(ext.at[:, mine, edge], ext.at[:, mine, edge], sems, 2, sib)
    corner_up = remote(ext.at[:, lift, edge], ext.at[:, below, edge], sems, 3, up)
    swap_below = remote(ext.at[:, below, body], ext.at[:, below, body], sems, 4, sib)
    swap_corner = remote(ext.at[:, below, edge], ext.at[:, below, edge], sems, 5, sib)

    def convert(rows):
        for plane in range(2):
            obj_ref[0, plane, rows, body] = field_ref[rows, plane, :].astype(BF16)

    def shifted(rows, start, width):
        for plane in range(2):
            value = obj_ref[0, plane, rows, pl.ds(start, width + LANES)].astype(F32)
            value = pltpu.roll(value, width + LANES - SHIFT, 1)[:, :width]
            obj_ref[1, plane, rows, pl.ds(start, width)] = value.astype(BF16)

    fetches[0].wait()
    convert(mine)

    @pl.when(has_left)
    def _():
        to_left.start()

    convert(other)

    @pl.when(has_up)
    def _():
        to_up.start()

    fetches[1].wait()
    for plane in range(2):
        planes_ref[plane] = probe_ref[:, plane, :]
    top, bottom = pl.ds(0, tile_r), pl.ds(tile_r, reach)
    shifted(top, 0, tile_c - LANES)
    acc_ref[0] = jnp.zeros(acc_ref.shape[1:], F32)

    @pl.when(has_right)
    def _():
        to_left.wait_recv()
        swap_edge.start()

    acc_ref[1] = jnp.zeros(acc_ref.shape[1:], F32)

    @pl.when(has_right)
    def _():
        swap_edge.wait_recv()

        @pl.when(has_up)
        def _():
            corner_up.start()

        shifted(top, tile_c - LANES, frame)

    @pl.when(has_down)
    def _():
        to_up.wait_recv()
        swap_below.start()
        swap_below.wait_recv()
        shifted(bottom, 0, tile_c - LANES)

    @pl.when(has_right & has_down)
    def _():
        corner_up.wait_recv()
        swap_corner.start()
        swap_corner.wait()
        shifted(bottom, tile_c - LANES, frame)

    @pl.when(has_right)
    def _():
        swap_edge.wait_send()

        @pl.when(has_up)
        def _():
            corner_up.wait_send()

    @pl.when(has_down)
    def _():
        swap_below.wait_send()

    @pl.when(has_left)
    def _():
        to_left.wait_send()

    @pl.when(has_up)
    def _():
        to_up.wait_send()

    for fetch in fetches[2:]:
        fetch.wait()


def halo(field, probe, extras, rows_n, cols_n):
    tile_r, planes, tile_c = field.shape
    frame = probe.shape[0]
    shape = (2, planes, tile_r + frame, tile_c + frame)
    in_vmem = pl.BlockSpec(memory_space=VMEM)
    return pl.pallas_call(
        functools.partial(halo_kernel, rows_n, cols_n, len(extras)),
        out_shape=(
            jax.ShapeDtypeStruct(shape, BF16),
            jax.ShapeDtypeStruct((planes, frame, frame), F32),
            jax.ShapeDtypeStruct(shape, F32),
            *(jax.ShapeDtypeStruct(x.shape, x.dtype) for x in extras),
        ),
        in_specs=[pl.BlockSpec(memory_space=pltpu.HBM)] * (2 + len(extras)),
        out_specs=(in_vmem,) * (3 + len(extras)),
        scratch_shapes=[
            VMEM(field.shape, F32),
            VMEM(probe.shape, F32),
            pltpu.SemaphoreType.DMA((2, 6)),
            pltpu.SemaphoreType.DMA((2 + len(extras),)),
        ],
        cost_estimate=pl.CostEstimate(flops=0, bytes_accessed=40 << 20, transcendentals=0),
        compiler_params=pltpu.CompilerParams(
            collective_id=0, has_side_effects=True, vmem_limit_bytes=8 << 20
        ),
        name="halo",
    )(*(pltpu.with_memory_space_constraint(x, pltpu.HBM) for x in (field, probe, *extras)))


def frames_kernel(
    row_ref, col_ref, count_ref, obj, probe_ref, amp_ref, first_ref, second_ref, _zero,
    acc, sum_ref, tall, wide, field,
):
    frame = probe_ref.shape[1]
    ext_rows, ext_cols = obj.shape[2:]
    top = lax.axis_index("row") * (ext_rows - frame)
    left = lax.axis_index("col") * (ext_cols - frame)
    step = 32
    sum_ref[...] = jnp.zeros_like(sum_ref)

    def one(slot, carry):
        row = row_ref[slot] - top
        col = col_ref[slot] - left
        odd = (col % LANES) // SHIFT
        cols = pl.ds(pl.multiple_of((col // LANES) * LANES, LANES), frame)
        for k in range(0, frame, step):
            rows = pl.ds(pl.multiple_of(row + k, step), step)
            o_re = obj[odd, 0, rows, cols].astype(F32)
            o_im = obj[odd, 1, rows, cols].astype(F32)
            p_re = probe_ref[0, k : k + step, :]
            p_im = probe_ref[1, k : k + step, :]
            tall[k : k + step, :] = (p_re * o_re - p_im * o_im).astype(BF16)
            tall[frame + k : frame + k + step, :] = (p_re * o_im + p_im * o_re).astype(BF16)
        half = jnp.dot(first_ref[...], tall[...], preferred_element_type=F32).astype(BF16)
        wide[:, :frame] = half[:frame]
        wide[:, frame:] = half[frame:]
        field[...] = jnp.dot(wide[...], second_ref[...], preferred_element_type=F32)
        for k in range(0, frame, step):
            f_re = field[k : k + step, :frame]
            f_im = field[k : k + step, frame:]
            amp = amp_ref[slot, k : k + step, :].astype(F32)
            power = f_re * f_re + f_im * f_im
            factor = amp * lax.rsqrt(jnp.maximum(power, FLOOR_SQUARED)) - 1.0
            tall[k : k + step, :] = (f_re * factor).astype(BF16)
            tall[frame + k : frame + k + step, :] = (f_im * factor).astype(BF16)
        half = jnp.dot(second_ref[...], tall[...], preferred_element_type=F32).astype(BF16)
        wide[:, :frame] = half[:frame]
        wide[:, frame:] = half[frame:]
        field[...] = jnp.dot(wide[...], first_ref[...], preferred_element_type=F32)
        for k in range(0, frame, step):
            rows = pl.ds(pl.multiple_of(row + k, step), step)
            here = pl.ds(k, step)
            x_re = field[k : k + step, :frame]
            x_im = field[k : k + step, frame:]
            o_re = obj[odd, 0, rows, cols].astype(F32)
            o_im = obj[odd, 1, rows, cols].astype(F32)
            p_re = probe_ref[0, k : k + step, :]
            p_im = probe_ref[1, k : k + step, :]
            acc[odd, 0, rows, cols] += p_re * x_re + p_im * x_im
            acc[odd, 1, rows, cols] += p_re * x_im - p_im * x_re
            sum_ref[0, here, :] += o_re * x_re + o_im * x_im
            sum_ref[1, here, :] += o_re * x_im - o_im * x_re
            sum_ref[2, here, :] += o_re * o_re + o_im * o_im
        return carry

    lax.fori_loop(0, count_ref[0], one, 0)
    for plane in range(2):
        for row in range(0, ext_rows - SHIFT, SHIFT):
            rows = pl.ds(row, SHIFT)
            acc[0, plane, rows, :] += pltpu.roll(acc[1, plane, rows, :], SHIFT, 1)


def frames(row_offset, col_offset, counts, obj, probe, amplitudes, first, second, acc):
    frame = probe.shape[1]
    in_vmem = pl.BlockSpec(memory_space=VMEM)
    in_smem = pl.BlockSpec(memory_space=pltpu.SMEM)
    return pl.pallas_call(
        frames_kernel,
        out_shape=(
            jax.ShapeDtypeStruct(acc.shape, F32),
            jax.ShapeDtypeStruct((3, frame, frame), F32),
        ),
        in_specs=[in_smem] * 3 + [in_vmem] * 6,
        out_specs=(in_vmem, in_vmem),
        input_output_aliases={8: 0},
        scratch_shapes=[
            VMEM((2 * frame, frame), BF16),
            VMEM((frame, 2 * frame), BF16),
            VMEM((frame, 2 * frame), F32),
        ],
        compiler_params=pltpu.CompilerParams(vmem_limit_bytes=10 << 20),
        name="frames",
    )(row_offset, col_offset, counts, obj, probe, amplitudes, first, second, acc)


def merge_kernel(
    rows_n, cols_n, with_probe, acc_ref, sum_ref, probe_ref, field_ref, share_ref, out_ref,
    fresh_ref, got, total, to_right, to_down, from_left, from_up,
    got_sum, part, col_got, row_part, row_got, sems, psems, asems,
):
    r = lax.axis_index("row")
    c = lax.axis_index("col")
    m = lax.axis_index("mode")
    half, _, tile_c = share_ref.shape
    tile_r = 2 * half
    frame = probe_ref.shape[1]
    near = frame - SHIFT - half
    upd_ref = acc_ref.at[0]
    has_up, has_down = r > 0, r < rows_n - 1
    has_left, has_right = c > 0, c < cols_n - 1
    whole = m == 0
    sib = {"mode": 1 - m}
    up, down = {"row": r - 1}, {"row": r + 1}
    left, right = {"col": c - 1}, {"col": c + 1}
    always = m >= 0
    row_peers = [{"row": lax.rem(r + d, rows_n)} for d in range(1, rows_n)]
    col_peers = [{"col": lax.rem(c + d, cols_n)} for d in range(1, cols_n)]
    if with_probe:
        greet([(always, p) for p in [sib] + row_peers + col_peers])
    else:
        greet([(always, sib), (has_up, up), (has_down, down), (has_left, left), (has_right, right)])

    def block(which, base):
        return pl.ds(pl.multiple_of(which * half + base, half), half)

    top_mine, low_mine = block(m, 0), block(m, tile_r)
    top_sib, low_sib = block(1 - m, 0), block(1 - m, tile_r)
    first_cols, body, edge = pl.ds(0, frame), pl.ds(0, tile_c), pl.ds(tile_c, frame)
    near_rows, far_rows = pl.ds(0, near), pl.ds(near, half - near)
    if with_probe:
        sum_rows = frame // 2
        col_rows = sum_rows // cols_n
        row_rows = col_rows // rows_n
        give = sum_ref.at[:, pl.ds(pl.multiple_of((1 - m) * sum_rows, sum_rows), sum_rows), :]
        swap_sum = remote(give, got_sum, psems, 0, sib)
        swap_sum.start()
    swap_low = remote(upd_ref.at[:, low_sib, :], got.at[1], sems, 0, sib)
    swap_low.start()
    swap_top = remote(upd_ref.at[:, top_sib, :], got.at[0], sems, 1, sib)
    swap_top.start()
    fall_near = remote(to_down.at[:, near_rows, :], from_up.at[:, near_rows, :], sems, 2, down)
    fall_far = remote(to_down.at[:, far_rows, :], from_up.at[:, far_rows, :], sems, 3, down)
    side = remote(to_right, from_left, sems, 4, right)

    if with_probe:
        swap_sum.wait_recv()
        at = pl.ds(pl.multiple_of(m * sum_rows, sum_rows), sum_rows)
        part[...] = sum_ref[:, at, :] + got_sum[...]
        col_copies = []
        for d in range(1, cols_n):
            there = lax.rem(c + d, cols_n)
            src = part.at[:, pl.ds(pl.multiple_of(there * col_rows, col_rows), col_rows), :]
            col_copies.append(remote(src, col_got.at[d - 1], psems, d, col_peers[d - 1]))
            col_copies[-1].start()
    swap_low.wait_recv()
    to_down[...] = (upd_ref[:, low_mine, :] + got[1]).astype(BF16)

    @pl.when(has_down)
    def _():
        fall_near.start()

        @pl.when(whole)
        def _():
            fall_far.start()

    swap_top.wait_recv()
    total[...] = upd_ref[:, top_mine, :] + got[0]
    peak = probe_ref[0] * probe_ref[0] + probe_ref[1] * probe_ref[1]
    peak = jnp.max(peak, keepdims=True) + EPSILON
    if with_probe:
        own = part[:, pl.ds(pl.multiple_of(c * col_rows, col_rows), col_rows), :]
        for d in range(1, cols_n):
            col_copies[d - 1].wait_recv()
            own = own + col_got[d - 1]
        row_part[...] = own
        row_copies = []
        for d in range(1, rows_n):
            there = lax.rem(r + d, rows_n)
            src = row_part.at[:, pl.ds(pl.multiple_of(there * row_rows, row_rows), row_rows), :]
            row_copies.append(remote(src, row_got.at[d - 1], psems, cols_n + d, row_peers[d - 1]))
            row_copies[-1].start()

    @pl.when(has_up)
    def _():
        fall_near.wait_recv()
        total[:, near_rows, :] += from_up[:, near_rows, :].astype(F32)

        @pl.when(whole)
        def _():
            fall_far.wait_recv()
            total[:, far_rows, :] += from_up[:, far_rows, :].astype(F32)

    @pl.when(has_right)
    def _():
        to_right[...] = total[:, :, edge].astype(BF16)
        side.start()

    spread = []
    if with_probe:
        own = row_part[:, pl.ds(pl.multiple_of(r * row_rows, row_rows), row_rows), :]
        for d in range(1, rows_n):
            row_copies[d - 1].wait_recv()
            own = own + row_got[d - 1]
        weight = own[2] + REGULARIZER

        def shard(row):
            start = m * sum_rows + c * col_rows + row * row_rows
            return pl.ds(pl.multiple_of(start, row_rows), row_rows)

        here = shard(r)
        fresh_ref[0, here, :] = probe_ref[0, here, :] + own[0] / weight
        fresh_ref[1, here, :] = probe_ref[1, here, :] + own[1] / weight

        def pass_on(back):
            ref = fresh_ref.at[:, shard(lax.rem(r + rows_n - back, rows_n)), :]
            for d in range(1, cols_n):
                slot = rows_n + back * cols_n + d
                copy = remote(ref, ref, asems, slot, col_peers[d - 1])
                copy.start()
                crossings.append(copy)

        crossings = []
        ref = fresh_ref.at[:, here, :]
        for d in range(1, rows_n):
            spread.append(remote(ref, ref, asems, d, row_peers[d - 1]))
            spread[-1].start()
        pass_on(0)
        for d in range(1, rows_n):
            spread[d - 1].wait_recv()
            pass_on(d)
    else:
        fresh_ref[...] = jnp.zeros_like(fresh_ref)

    @pl.when(has_left)
    def _():
        side.wait_recv()
        total[:, :, first_cols] += from_left[...].astype(F32)

    for plane in range(2):
        share_ref[:, plane, :] = field_ref[top_mine, plane, :] + total[plane, :, body] / peak

    if with_probe:
        for copy in crossings:
            copy.wait_recv()
        ref = fresh_ref.at[:, at, :]
        last = remote(ref, ref, asems, 0, sib)
        last.start()
        for plane in range(2):
            out_ref[at, plane, :] = fresh_ref[plane, at, :]

    swap_low.wait_send()
    swap_top.wait_send()

    @pl.when(has_right)
    def _():
        side.wait_send()

    @pl.when(has_down)
    def _():
        fall_near.wait_send()

        @pl.when(whole)
        def _():
            fall_far.wait_send()

    if with_probe:
        swap_sum.wait_send()
        for copy in col_copies + row_copies + spread + crossings:
            copy.wait_send()
        last.wait()
        off = pl.ds(pl.multiple_of((1 - m) * sum_rows, sum_rows), sum_rows)
        for plane in range(2):
            out_ref[off, plane, :] = fresh_ref[plane, off, :]
    else:
        for plane in range(2):
            out_ref[:, plane, :] = fresh_ref[plane]


def merge(acc, sums, probe, field, rows_n, cols_n, with_probe):
    tile_r, _, tile_c = field.shape
    frame = probe.shape[1]
    half = tile_r // 2
    ext_c = tile_c + frame
    sum_rows = frame // 2
    if with_probe:
        col_rows = sum_rows // cols_n
        row_rows = col_rows // rows_n
    else:
        col_rows = row_rows = 8
    in_vmem = pl.BlockSpec(memory_space=VMEM)
    return pl.pallas_call(
        functools.partial(merge_kernel, rows_n, cols_n, with_probe),
        out_shape=(
            jax.ShapeDtypeStruct((half, 2, tile_c), F32),
            jax.ShapeDtypeStruct((frame, 2, frame), F32),
        ),
        in_specs=[in_vmem] * 4,
        out_specs=(in_vmem, in_vmem),
        scratch_shapes=[
            VMEM((2, frame, frame), F32),
            VMEM((2, 2, half, ext_c), F32),
            VMEM((2, half, ext_c), F32),
            VMEM((2, half, frame), BF16),
            VMEM((2, half, ext_c), BF16),
            VMEM((2, half, frame), BF16),
            VMEM((2, half, ext_c), BF16),
            VMEM((3, sum_rows, frame), F32),
            VMEM((3, sum_rows, frame), F32),
            VMEM((max(1, cols_n - 1), 3, col_rows, frame), F32),
            VMEM((3, col_rows, frame), F32),
            VMEM((max(1, rows_n - 1), 3, row_rows, frame), F32),
            pltpu.SemaphoreType.DMA((2, 5)),
            pltpu.SemaphoreType.DMA((2, rows_n + cols_n)),
            pltpu.SemaphoreType.DMA((2, rows_n + rows_n * cols_n)),
        ],
        compiler_params=pltpu.CompilerParams(
            collective_id=1, has_side_effects=True, vmem_limit_bytes=14 << 20
        ),
        name="merge",
    )(acc, sums, probe, field)


def body(rows_n, cols_n, object_field, probe_field, amplitudes, row_offset, col_offset, counts):
    frame = probe_field.shape[0]
    first, second = dft_tables(frame)
    extras = (row_offset, col_offset, amplitudes, first, second)
    obj, probe, acc, *extras = halo(object_field, probe_field, extras, rows_n, cols_n)
    rows, cols, amplitudes, first, second = extras
    acc, sums = frames(rows, cols, counts, obj, probe, amplitudes, first, second, acc)
    with_probe = frame % (2 * rows_n * cols_n * 8) == 0
    object_new, fresh = merge(acc, sums, probe, object_field, rows_n, cols_n, with_probe)
    if not with_probe:
        sums = lax.psum(sums, ("row", "col", "mode"))
        fresh = probe + sums[:2] / (sums[2:] + REGULARIZER)
        fresh = jnp.moveaxis(fresh, 0, 1)
    return (object_new, fresh)


def solution(mesh):
    split = ("groups", "row", "col", "mode")
    placed = (
        P(("groups", "row"), None, "col"),
        P("groups", None, None),
        P(split, None, None),
        P(split),
        P(split),
        P(split),
    )
    return jax.shard_map(
        functools.partial(body, mesh.shape["row"], mesh.shape["col"]),
        mesh=mesh,
        in_specs=placed,
        out_specs=(P(("groups", "row", "mode"), None, "col"), P("groups", None, None)),
        check_vma=False,
    )
```
